128 devices in a mesh: row: 8 (over x, z_lo), col: 16 (over z_hi, y, core).
Axes of the slice: x: 4, y: 4, z: 4 (z_hi: 2, z_lo: 2; z = z_hi * 2 + z_lo), core: 2. Of those that a mesh axis runs over, the one named last changes fastest.
Arguments:
- amplitudes: bfloat16 [32, 768, 768], P('row', 'col'), may hold values from -6 to 6
- factors: bfloat16 [64, 768, 768], P('col', 'row'), may hold values from -0.109375 to 0.109375
- counts: int32 [8], replicated, may hold values from 1 to 4, 16 in all
- pair_index: int32 [32, 2], replicated, may hold values from 0 to 23
- occ_energy: float32 [24], replicated, may hold values from -2 to -0.5
- vir_energy: float32 [768], replicated, may hold values from 0.5 to 3
Outputs:
- new_amplitudes: bfloat16 [32, 768, 768], P('row', 'col')
The draws below stay inside these ranges and needn't reach their ends.
Inputs may be any that keep to these rules, and one draw needn't show every extreme that they name: The counts sum to 2 times the number of owner rows. `pair_index`: entries of slots that are not live are not used.
All inputs are finite; a program needn't handle non-finite values.
Results may differ from the reference program's by a relative error of at most 0.0046.
Values may be sent and summed in bfloat16 or wider, within the bound.
No kernel may reach another device: no remote copies, remote signals or barrier semaphores. Data moves between devices by JAX's collectives and lax.ppermute only.
A program may use at most 64 MiB of HBM per device.

```python
import math
import jax
import jax.numpy as jnp
import numpy as np
from jax import lax

V = 768
NOCC = 24
WORK = 2
SLOTS = 4
NQ = 64
N_ROW = 8


def set_ends(array, rng, low, high):
    place = [jax.random.randint(jax.random.fold_in(rng, axis), (), 0, length) for axis, length in enumerate(array.shape)]
    main_axis = array.shape.index(max(array.shape))
    neighbour = place[:main_axis] + [(place[main_axis] + 1) % array.shape[main_axis]] + place[main_axis + 1:]
    return array.at[tuple(place)].set(low).at[tuple(neighbour)].set(high)


def levels(rng, dims, cuts, low, high):
    def one(position, shards_of):
        draws = jax.random.uniform(jax.random.fold_in(jax.random.fold_in(rng, 6), position), (shards_of,), jnp.float32, low / len(cuts), high / len(cuts))
        return jnp.repeat(jnp.exp(draws), dims[position] // shards_of).reshape((-1,) + (1,) * (len(dims) - position - 1))

    loudness = one(*cuts[0])
    for cut in cuts[1:]:
        loudness = loudness * one(*cut)
    return loudness


def profile(number_of, total, reach, lean):
    loads = [(1 << 20) // math.isqrt(grade ** lean) + 1 for grade in range(2, number_of + 1)]
    rest, given = total - reach - (number_of - 1), [1] * (number_of - 1)
    while rest > 0:
        movable = [i for i in range(number_of - 1) if given[i] < reach]
        mass, remaining = sum([loads[i] for i in movable]), rest
        for i in movable:
            addition = min(reach - given[i], max(1, remaining * loads[i] // mass), rest)
            given[i] = given[i] + addition
            rest = rest - addition
    return np.array([reach] + given)


def ragged(stream_key, number_of, total, bound, skew):
    if number_of == 2:
        one = jax.random.randint(stream_key, (), max(1, total - bound), min(bound, total - 1) + 1)
        return jnp.stack([one, total - one])
    tallies = jnp.asarray(profile(number_of, total, bound, skew), jnp.int32)
    couples = (number_of - 1) // 2
    source_of, receiver = tallies[1:1 + 2 * couples:2], tallies[2:2 + 2 * couples:2]
    margin = jnp.minimum(source_of - 1, bound - receiver)
    shifted = jax.random.randint(jax.random.fold_in(stream_key, 1), (couples,), 0, 1 << 20) % (margin + 1)
    tallies = tallies.at[1:1 + 2 * couples:2].set(source_of - shifted).at[2:2 + 2 * couples:2].set(receiver + shifted)
    return tallies[jax.random.permutation(jax.random.fold_in(stream_key, 2), number_of)]


def gaussian(own_key, dims, spread, most, split=(), kind=jnp.bfloat16):
    entries = jax.random.normal(own_key, dims, jnp.float32) * spread
    if len(split) > 0:
        entries = levels(own_key, dims, split, -0.22, 0.18) * entries
    return jnp.clip(entries, min=-most, max=most).astype(kind)


def setup_inputs(seed: int = 0) -> dict:
    keys = jax.random.split(jax.random.key(seed), 7)
    amplitudes = gaussian(keys[0], (N_ROW * SLOTS, V, V), 1.0, 6.0, ((0, 8), (1, 16)))
    factors = gaussian(keys[1], (NQ, V, V), (4 * V) ** -0.5, 0.109375, ((0, 16), (1, 8)))
    counts = ragged(keys[2], N_ROW, WORK * N_ROW, SLOTS, 2).astype(jnp.int32)
    pair_index = set_ends(jax.random.randint(keys[3], (N_ROW * SLOTS, 2), 0, NOCC), jax.random.fold_in(keys[3], 1), 0, NOCC - 1).astype(jnp.int32)
    occ_energy = jnp.clip(jax.random.uniform(keys[4], (NOCC,), jnp.float32, -2.0, -0.5), -2.0, -0.5)
    vir_energy = jnp.clip(jax.random.uniform(keys[5], (V,), jnp.float32, 0.5, 3.0), 0.5, 3.0)
    return {"amplitudes": amplitudes, "factors": factors, "counts": counts, "pair_index": pair_index, "occ_energy": occ_energy, "vir_energy": vir_energy}


level_shift = 1.0


def reference(amplitudes, factors, counts, pair_index, occ_energy, vir_energy):
    total_slots = amplitudes.shape[0]
    slot_ids = jnp.arange(total_slots, dtype=jnp.int32)
    owner_rows = slot_ids // SLOTS
    is_live = (slot_ids % SLOTS) < counts[owner_rows]
    pair_energy = occ_energy[pair_index[:, 0]] + occ_energy[pair_index[:, 1]]
    base = vir_energy[:, None] + vir_energy[None, :]
    factor_float = factors.astype(jnp.float32)

    def single_pair(packed):
        amps, energy, alive = packed
        amps_float = amps.astype(jnp.float32)
        halfway = jnp.einsum("cb,qdb->qcd", amps_float, factor_float).astype(jnp.bfloat16)
        ladder = jnp.einsum("qac,qcd->ad", factor_float, halfway.astype(jnp.float32))
        denominator = base - energy
        updated = amps_float - (ladder + denominator * amps_float) / (denominator + level_shift)
        return jnp.where(alive, updated, 0.0).astype(jnp.bfloat16)

    return lax.map(single_pair, (amplitudes, pair_energy, is_live))
```

```python
import functools
import itertools

import jax
import jax.numpy as jnp
from jax import lax
from jax.experimental import pallas as pl
from jax.experimental.pallas import tpu as pltpu
from jax.sharding import PartitionSpec as P

level_shift = 1.0

DEVICES = list(itertools.product(range(4), range(4), range(2), range(2), range(2)))


def position(x, y, zh, zl, k):
    return (x * 2 + zl) * 16 + zh * 8 + y * 2 + k


def shift(array, dx=0, dy=0, dzh=0, dzl=0, dk=0):
    pairs = [
        (position(x, y, zh, zl, k), position(x ^ dx, y ^ dy, zh ^ dzh, zl ^ dzl, k ^ dk))
        for x, y, zh, zl, k in DEVICES
    ]
    return lax.ppermute(array, ("row", "col"), pairs)


def gather_factors(own):
    x1 = shift(own, dx=1)
    x3 = shift(own, dx=3)
    z1 = shift(own, dzl=1)
    x2 = jnp.concatenate([shift(x3[:2], dx=1), shift(x1[2:], dx=3)])
    x1z1 = shift(z1, dx=1)
    x3z1 = shift(z1, dx=3)
    x2z1 = shift(x2, dzl=1)
    return own, z1, x1, x1z1, x2, x2z1, x3, x3z1


def gather_item(own):
    pair = jnp.stack([own, shift(own, dzh=1)])
    ys = jnp.stack([pair] + [shift(pair, dy=i) for i in (1, 2, 3)])
    return jnp.stack([ys, shift(ys, dk=1)]).reshape((16,) + own.shape)


def ladder_kernel(where, amps, *refs):
    blocks = refs[:8]
    keep, send = refs[8:10]
    amps_v, fac_v, acc, amp_sem, fac_sem = refs[10:]
    row, y, zh, k = where[0], where[1], where[2], where[3]
    amp_copies = []
    for index in range(16):
        dk, dy, dzh = index // 8, (index // 2) % 4, index % 2
        at = ((zh ^ dzh) * 8 + (y ^ dy) * 2 + (k ^ dk)) * 48
        amp_copies.append(
            pltpu.make_async_copy(amps.at[index], amps_v.at[pl.ds(pl.multiple_of(at, 16), 48), :], amp_sem.at[index])
        )
    fac_copies = []
    for q in range(4):
        for j in range(8):
            at = (row ^ j) * 96
            fac_copies.append(
                pltpu.make_async_copy(
                    blocks[j].at[q], fac_v.at[q, pl.ds(pl.multiple_of(at, 32), 96), :], fac_sem.at[q, j]
                )
            )
    for copy in amp_copies + fac_copies:
        copy.start()
    for copy in amp_copies:
        copy.wait()
    for q in range(4):
        for j in range(8):
            fac_copies[q * 8 + j].wait()
        factor = fac_v[q]
        halfway = lax.dot_general(
            amps_v[...], factor, (((1,), (1,)), ((), ())), preferred_element_type=jnp.float32
        ).astype(jnp.bfloat16)
        part = jnp.dot(factor, halfway, preferred_element_type=jnp.float32)
        if q == 0:
            acc[...] = part
        else:
            acc[...] += part
    for b in range(8):
        to = ((b % 4) ^ y) * 2 + ((b // 4) ^ zh)
        keep[to] = acc[pl.ds(pl.multiple_of(b * 96 + k * 48, 16), 48), :]
        send[to] = acc[pl.ds(pl.multiple_of(b * 96 + (1 - k) * 48, 16), 48), :].astype(jnp.bfloat16)


def ladder_item(where, amps, blocks):
    any_spec = pl.BlockSpec(memory_space=pl.ANY)
    vmem = pl.BlockSpec(memory_space=pltpu.VMEM)
    return pl.pallas_call(
        ladder_kernel,
        out_shape=(
            jax.ShapeDtypeStruct((8, 48, 768), jnp.float32),
            jax.ShapeDtypeStruct((8, 48, 768), jnp.bfloat16),
        ),
        in_specs=[pl.BlockSpec(memory_space=pltpu.SMEM)] + [any_spec] * 9,
        out_specs=(vmem, vmem),
        scratch_shapes=[
            pltpu.VMEM((768, 768), jnp.bfloat16),
            pltpu.VMEM((4, 768, 768), jnp.bfloat16),
            pltpu.VMEM((768, 768), jnp.float32),
            pltpu.SemaphoreType.DMA((16,)),
            pltpu.SemaphoreType.DMA((4, 8)),
        ],
        compiler_params=pltpu.CompilerParams(vmem_limit_bytes=40 << 20),
    )(where, amps, *blocks)


def reduce_item(keep, send):
    total = keep + shift(send, dk=1).astype(jnp.float32)
    out = total[2:].astype(jnp.bfloat16)
    mine = total[:2]
    for i in (1, 2, 3):
        mine = mine + shift(out[2 * i - 2:2 * i], dy=i).astype(jnp.float32)
    return mine[0] + shift(mine[1].astype(jnp.bfloat16), dzh=1).astype(jnp.float32)


def pick(table, index):
    hit = jnp.arange(table.shape[0], dtype=jnp.int32) == index
    return jnp.sum(jnp.where(hit, table, 0))


def per_device(amplitudes, factors, counts, pair_index, occ_energy, vir_energy):
    row = lax.axis_index("row").astype(jnp.int32)
    col = lax.axis_index("col").astype(jnp.int32)
    zh, y, k = col // 8, (col // 2) % 4, col % 2
    where = jnp.stack([row, y, zh, k]).astype(jnp.int32)

    rows = jnp.arange(8, dtype=jnp.int32)
    extra = jnp.maximum(counts - 2, 0)
    spare = jnp.maximum(2 - counts, 0)
    below = rows[:, None] > rows[None, :]
    extra_from = jnp.sum(jnp.where(below, extra[None, :], 0), axis=1)
    spare_from = jnp.sum(jnp.where(below, spare[None, :], 0), axis=1)
    my_count = pick(counts, row)
    my_extra_from = pick(extra_from, row)
    my_spare_from = pick(spare_from, row)
    source = jnp.sum((extra_from + extra <= my_spare_from).astype(jnp.int32))
    source_slot = 2 + my_spare_from - pick(extra_from, source)
    borrowed = my_count < 2

    blocks = gather_factors(factors)
    amps_0 = gather_item(amplitudes[0])

    received = []
    for j in range(1, 8):
        there = row ^ j
        late = pick(spare_from, there) - my_extra_from == 1
        chosen = jnp.where(late, amplitudes[3], amplitudes[2])
        received.append(shift(chosen, dx=j >> 1, dzl=j & 1))
    item_1 = amplitudes[1]
    for j in range(1, 8):
        item_1 = jnp.where(borrowed & (source == row ^ j), received[j - 1], item_1)
    amps_1 = gather_item(item_1)

    keep_1, send_1 = ladder_item(where, amps_1, blocks)
    keep_0, send_0 = ladder_item(where, amps_0, blocks)
    ladder_1 = reduce_item(keep_1, send_1)
    ladder_0 = reduce_item(keep_0, send_0)

    row_energy = lax.dynamic_slice_in_dim(vir_energy, col * 48, 48, 0)
    virtual = row_energy[:, None] + vir_energy[None, :]

    def finish(amps, ladder, slot):
        ids = jnp.arange(32, dtype=jnp.int32)[:, None]
        pair = jnp.sum(jnp.where(ids == slot, pair_index, 0), axis=0)
        occupied = jnp.arange(occ_energy.shape[0], dtype=jnp.int32)
        picks = (pair[:, None] == occupied[None, :]).astype(jnp.float32)
        denominator = virtual - jnp.sum(picks * occ_energy[None, :])
        t = amps.astype(jnp.float32)
        return (t - (ladder + denominator * t) / (denominator + level_shift)).astype(jnp.bfloat16)

    slot_1 = jnp.where(borrowed, source * 4 + source_slot, row * 4 + 1)
    done_1 = finish(item_1, ladder_1, slot_1)
    done_0 = finish(amplitudes[0], ladder_0, row * 4)

    zero = jnp.zeros_like(done_0)
    returned = [shift(done_1, dx=j >> 1, dzl=j & 1) for j in range(1, 8)]
    slots = [done_0, jnp.where(borrowed, zero, done_1)]
    for s in (2, 3):
        wanted = my_extra_from + (s - 2)
        helper = jnp.sum((spare_from + spare <= wanted).astype(jnp.int32))
        slot = zero
        for j in range(1, 8):
            slot = jnp.where((my_count > s) & (helper == row ^ j), returned[j - 1], slot)
        slots.append(slot)
    return jnp.stack(slots)


def solution(mesh):
    in_specs = (P("row", "col", None), P("col", "row", None), P(), P(), P(), P())
    out_specs = P("row", "col", None)
    return jax.shard_map(
        per_device, mesh=mesh, in_specs=in_specs, out_specs=out_specs, check_vma=False
    )
```

```python
import itertools

import jax
import jax.numpy as jnp
from jax import lax
from jax.experimental import pallas as pl
from jax.experimental.pallas import tpu as pltpu
from jax.sharding import PartitionSpec as P

level_shift = 1.0

DEVICES = list(itertools.product(range(4), range(4), range(2), range(2), range(2)))
BF16, F32, I32 = jnp.bfloat16, jnp.float32, jnp.int32
TILE = (48, 768)


def position(x, y, zh, zl, k):
    return (x * 2 + zl) * 16 + zh * 8 + y * 2 + k


def shift(array, dx=0, dy=0, dzh=0, dzl=0, dk=0):
    pairs = [
        (position(x, y, zh, zl, k), position(x ^ dx, y ^ dy, zh ^ dzh, zl ^ dzl, k ^ dk))
        for x, y, zh, zl, k in DEVICES
    ]
    return lax.ppermute(array, ("row", "col"), pairs)


def call(kernel, outs, args, scratch=(), smem=0):
    spaces = [pltpu.SMEM] * smem + [pltpu.VMEM] * (len(args) - smem)
    return pl.pallas_call(
        kernel,
        out_shape=tuple(jax.ShapeDtypeStruct(s, d) for s, d in outs),
        in_specs=[pl.BlockSpec(memory_space=space) for space in spaces],
        out_specs=tuple(pl.BlockSpec(memory_space=pltpu.VMEM) for _ in outs),
        scratch_shapes=list(scratch),
        compiler_params=pltpu.CompilerParams(vmem_limit_bytes=40 << 20),
    )(*args)


def here():
    row = lax.axis_index("row").astype(I32)
    col = lax.axis_index("col").astype(I32)
    return row, col, (col // 2) % 4, col // 8, col % 2


def choose(values, index):
    out = values[0]
    for i in range(1, len(values)):
        out = jnp.where(index == i, values[i], out)
    return out


class Plan:
    def __init__(self, counts):
        self.count = [counts[i] for i in range(8)]
        self.extra = [jnp.maximum(c - 2, 0) for c in self.count]
        self.spare = [jnp.maximum(2 - c, 0) for c in self.count]
        self.extra_from, self.spare_from = [jnp.int32(0)], [jnp.int32(0)]
        for i in range(7):
            self.extra_from.append(self.extra_from[i] + self.extra[i])
            self.spare_from.append(self.spare_from[i] + self.spare[i])

    def borrows(self, row):
        return choose(self.count, row) < 2

    def source(self, row):
        wanted = choose(self.spare_from, row)
        owner = jnp.int32(0)
        for i in range(8):
            owner += (self.extra_from[i] + self.extra[i] <= wanted).astype(I32)
        owner = jnp.minimum(owner, 7)
        return owner, 2 + wanted - choose(self.extra_from, owner)

    def helper(self, row, slot):
        wanted = choose(self.extra_from, row) + (slot - 2)
        worker = jnp.int32(0)
        for i in range(8):
            worker += (self.spare_from[i] + self.spare[i] <= wanted).astype(I32)
        return jnp.minimum(worker, 7)


def offer_kernel(counts, amps, *outs):
    plan = Plan(counts)
    row = here()[0]
    for j in range(8):
        late = choose(plan.spare_from, row ^ j) - choose(plan.extra_from, row) == 1
        outs[j // 2][j % 2] = jnp.where(late, amps[3], amps[2])


def relay_kernel(counts, *refs):
    out = refs[4]
    plan = Plan(counts)
    row = here()[0]
    step = (plan.source(row ^ 1)[0] ^ row) >> 1
    for dx in range(4):
        @pl.when(step == dx)
        def _():
            out[...] = refs[dx][1]


def accept_kernel(counts, amps, relayed, *refs):
    out = refs[4]
    plan = Plan(counts)
    row = here()[0]
    source = plan.source(row)[0] ^ row
    borrows = plan.borrows(row)
    out[...] = jnp.where(borrows, relayed[...], amps[1])
    for dx in range(4):
        @pl.when(borrows & (source == 2 * dx))
        def _():
            out[...] = refs[dx][0]


def borrow(counts, amplitudes):
    offers = call(offer_kernel, [((2,) + TILE, BF16)] * 4, (counts, amplitudes), smem=1)
    got = [offers[0]] + [shift(offers[dx], dx=dx) for dx in (1, 2, 3)]
    relayed = shift(call(relay_kernel, [(TILE, BF16)], (counts, *got), smem=1)[0], dzl=1)
    return call(accept_kernel, [(TILE, BF16)], (counts, amplitudes, relayed, *got), smem=1)[0]


def gather_factors(own):
    x1 = shift(own, dx=1)
    x3 = shift(own, dx=3)
    z1 = shift(own, dzl=1)
    x2 = jnp.concatenate([shift(x3[:2], dx=1), shift(x1[2:], dx=3)])
    x1z1 = shift(z1, dx=1)
    x3z1 = shift(z1, dx=3)
    x2z1 = shift(x2, dzl=1)
    return own, z1, x1, x1z1, x2, x2z1, x3, x3z1


def gather_item(own):
    pair = jnp.stack([own, shift(own, dzh=1)])
    ys = [pair] + [shift(pair, dy=i) for i in (1, 2, 3)]
    return ys + [shift(piece, dk=1) for piece in ys]


def ladder_kernel(*refs):
    pieces, blocks = refs[:8], refs[8:16]
    keep, send, amps_v, fac_v, acc = refs[16:]
    row, _, y, zh, k = here()
    for dk in range(2):
        for dy in range(4):
            for dz in range(2):
                at = ((zh ^ dz) * 8 + (y ^ dy) * 2 + (k ^ dk)) * 48
                amps_v[pl.ds(pl.multiple_of(at, 16), 48), :] = pieces[dk * 4 + dy][dz]
    for q in range(4):
        for j in range(8):
            fac_v[q, pl.ds(pl.multiple_of((row ^ j) * 96, 32), 96), :] = blocks[j][q]
        factor = fac_v[q]
        halfway = lax.dot_general(
            amps_v[...], factor, (((1,), (1,)), ((), ())), preferred_element_type=F32
        ).astype(BF16)
        part = jnp.dot(factor, halfway, preferred_element_type=F32)
        if q == 0:
            acc[...] = part
        else:
            acc[...] += part
    for b in range(8):
        to = ((b % 4) ^ y) * 2 + ((b // 4) ^ zh)
        keep[to] = acc[pl.ds(pl.multiple_of(b * 96 + k * 48, 16), 48), :]
        send[to] = acc[pl.ds(pl.multiple_of(b * 96 + (1 - k) * 48, 16), 48), :].astype(BF16)


def ladder_item(pieces, blocks):
    scratch = [pltpu.VMEM((768, 768), BF16), pltpu.VMEM((4, 768, 768), BF16), pltpu.VMEM((768, 768), F32)]
    return call(ladder_kernel, [((8,) + TILE, F32), ((8,) + TILE, BF16)], (*pieces, *blocks), scratch)


def core_kernel(keep, got, mine, y1, y2, y3):
    mine[...] = keep[:2] + got[:2].astype(F32)
    for i, out in ((1, y1), (2, y2), (3, y3)):
        out[...] = (keep[2 * i:2 * i + 2] + got[2 * i:2 * i + 2].astype(F32)).astype(BF16)


def ring_kernel(mine, y1, y2, y3, left, out):
    total = mine[...] + y1[...].astype(F32) + y2[...].astype(F32) + y3[...].astype(F32)
    left[...] = total[0]
    out[...] = total[1].astype(BF16)


def reduce_item(keep, send):
    pair = (2,) + TILE
    mine, *outs = call(core_kernel, [(pair, F32)] + [(pair, BF16)] * 3, (keep, shift(send, dk=1)))
    ys = [shift(out, dy=i + 1) for i, out in enumerate(outs)]
    left, out = call(ring_kernel, [(TILE, F32), (TILE, BF16)], (mine, *ys))
    return left, shift(out, dzh=1)


def finish_kernel(which, counts, pairs, occ, vir, amps, left, got, out):
    row, col, *_ = here()
    slot = row * 4
    if which == 1:
        plan = Plan(counts)
        owner, place = plan.source(row)
        slot = jnp.where(plan.borrows(row), owner * 4 + place, slot + 1)
    energy = occ[pairs[slot, 0]] + occ[pairs[slot, 1]]
    across = jnp.broadcast_to(vir[...], TILE)
    lane = lax.broadcasted_iota(I32, TILE, 1)
    mine = lane - lax.broadcasted_iota(I32, TILE, 0) == col * 48
    down = jnp.sum(jnp.where(mine, across, 0.0), axis=1, keepdims=True)
    denominator = (down + across) - energy
    t = amps[...].astype(F32)
    ladder = left[...] + got[...].astype(F32)
    out[...] = (t - (ladder + denominator * t) / (denominator + level_shift)).astype(BF16)


def place_kernel(counts, done_0, done_1, *refs):
    out = refs[7]
    plan = Plan(counts)
    row = here()[0]
    count = choose(plan.count, row)
    zero = jnp.zeros(TILE, BF16)
    out[0] = done_0[...]
    out[1] = jnp.where(count >= 2, done_1[...], zero)
    for slot in (2, 3):
        out[slot] = zero
        worker = plan.helper(row, slot) ^ row
        for j in range(1, 8):
            @pl.when((count > slot) & (worker == j))
            def _():
                out[slot] = refs[j - 1][...]


def per_device(amplitudes, factors, counts, pair_index, occ_energy, vir_energy):
    vir = vir_energy.reshape(1, 768)
    item_0 = amplitudes[0]
    item_1 = borrow(counts, amplitudes)
    blocks = gather_factors(factors)
    pieces_0 = gather_item(item_0)
    pieces_1 = gather_item(item_1)
    parts_1 = ladder_item(pieces_1, blocks)
    parts_0 = ladder_item(pieces_0, blocks)
    sums_1 = reduce_item(*parts_1)
    sums_0 = reduce_item(*parts_0)

    def finish(which, amps, sums):
        kernel = lambda *refs: finish_kernel(which, *refs)
        args = (counts, pair_index, occ_energy, vir, amps, *sums)
        return call(kernel, [(TILE, BF16)], args, smem=3)[0]

    done_1 = finish(1, item_1, sums_1)
    returned = [shift(done_1, dx=j >> 1, dzl=j & 1) for j in range(1, 8)]
    done_0 = finish(0, item_0, sums_0)
    return call(place_kernel, [((4,) + TILE, BF16)], (counts, done_0, done_1, *returned), smem=1)[0]


def solution(mesh):
    in_specs = (P("row", "col", None), P("col", "row", None), P(), P(), P(), P())
    out_specs = P("row", "col", None)
    return jax.shard_map(
        per_device, mesh=mesh, in_specs=in_specs, out_specs=out_specs, check_vma=False
    )
```

```python
import itertools

import jax
import jax.numpy as jnp
from jax import lax
from jax.experimental import pallas as pl
from jax.experimental.pallas import tpu as pltpu
from jax.sharding import PartitionSpec as P


level_shift = 1.0

DEVICES = list(itertools.product(range(4), range(4), range(2), range(2), range(2)))
BF16, F32, I32 = jnp.bfloat16, jnp.float32, jnp.int32
TILE = (48, 768)


def position(x, y, zh, zl, k):
    return (x * 2 + zl) * 16 + zh * 8 + y * 2 + k


def shift(array, dx=0, dy=0, dzh=0, dzl=0, dk=0):
    pairs = [
        (position(x, y, zh, zl, k), position(x ^ dx, y ^ dy, zh ^ dzh, zl ^ dzl, k ^ dk))
        for x, y, zh, zl, k in DEVICES
    ]
    return lax.ppermute(array, ("row", "col"), pairs)


def call(kernel, outs, args, scratch=(), smem=0):
    spaces = [pltpu.SMEM] * smem + [pltpu.VMEM] * (len(args) - smem)
    return pl.pallas_call(
        kernel,
        out_shape=tuple(jax.ShapeDtypeStruct(s, d) for s, d in outs),
        in_specs=[pl.BlockSpec(memory_space=space) for space in spaces],
        out_specs=tuple(pl.BlockSpec(memory_space=pltpu.VMEM) for _ in outs),
        scratch_shapes=list(scratch),
        compiler_params=pltpu.CompilerParams(vmem_limit_bytes=40 << 20),
    )(*args)


def here():
    row = lax.axis_index("row").astype(I32)
    col = lax.axis_index("col").astype(I32)
    return row, col, (col // 2) % 4, col // 8, col % 2


def choose(values, index):
    out = values[0]
    for i in range(1, len(values)):
        out = jnp.where(index == i, values[i], out)
    return out


class Plan:
    def __init__(self, counts):
        self.count = [counts[i] for i in range(8)]
        self.extra = [jnp.maximum(c - 2, 0) for c in self.count]
        self.spare = [jnp.maximum(2 - c, 0) for c in self.count]
        self.extra_from, self.spare_from = [jnp.int32(0)], [jnp.int32(0)]
        for i in range(7):
            self.extra_from.append(self.extra_from[i] + self.extra[i])
            self.spare_from.append(self.spare_from[i] + self.spare[i])

    def borrows(self, row):
        return choose(self.count, row) < 2

    def source(self, row):
        wanted = choose(self.spare_from, row)
        owner = jnp.int32(0)
        for i in range(8):
            owner += (self.extra_from[i] + self.extra[i] <= wanted).astype(I32)
        owner = jnp.minimum(owner, 7)
        return owner, 2 + wanted - choose(self.extra_from, owner)

    def helper(self, row, slot):
        wanted = choose(self.extra_from, row) + (slot - 2)
        worker = jnp.int32(0)
        for i in range(8):
            worker += (self.spare_from[i] + self.spare[i] <= wanted).astype(I32)
        return jnp.minimum(worker, 7)


def offer_kernel(counts, amps, *outs):
    plan = Plan(counts)
    row = here()[0]
    for j in range(8):
        late = choose(plan.spare_from, row ^ j) - choose(plan.extra_from, row) == 1
        outs[j // 2][j % 2] = jnp.where(late, amps[3], amps[2])


def relay_kernel(counts, amps, *refs):
    got, (relayed, mine) = refs[:4], refs[4:]
    plan = Plan(counts)
    row = here()[0]
    step = (plan.source(row ^ 1)[0] ^ row) >> 1
    source = plan.source(row)[0] ^ row
    borrows = plan.borrows(row)
    mine[...] = amps[1]
    for dx in range(4):
        @pl.when(step == dx)
        def _():
            relayed[...] = got[dx][1]

        @pl.when(borrows & (source == 2 * dx))
        def _():
            mine[...] = got[dx][0]


def accept_kernel(counts, mine, beside, relayed, relayed_beside, pair):
    plan = Plan(counts)
    row = here()[0]
    far = plan.borrows(row) & (((plan.source(row)[0] ^ row) & 1) == 1)
    pair[0] = jnp.where(far, relayed[...], mine[...])
    pair[1] = jnp.where(far, relayed_beside[...], beside[...])


def borrow(counts, amplitudes):
    offers = call(offer_kernel, [((2,) + TILE, BF16)] * 4, (counts, amplitudes), smem=1)
    got = [offers[0]] + [shift(offers[dx], dx=dx) for dx in (1, 2, 3)]
    relayed, mine = call(relay_kernel, [(TILE, BF16)] * 2, (counts, amplitudes, *got), smem=1)
    near = shift(relayed, dzl=1)
    beside = shift(mine, dzh=1)
    far = shift(relayed, dzl=1, dzh=1)
    return call(accept_kernel, [((2,) + TILE, BF16)], (counts, mine, beside, near, far), smem=1)[0]


def gather_factors(own):
    x3_low = shift(own[:2], dx=3)
    x1_high = shift(own[2:], dx=1)
    z1 = shift(own, dzl=1)
    x2 = shift(x3_low, dx=1), shift(x1_high, dx=3)
    x1_low = shift(own[:2], dx=1)
    x3_high = shift(own[2:], dx=3)
    x1z1 = shift(z1, dx=1)
    x3z1 = shift(z1, dx=3)
    x2z1 = shift(jnp.concatenate(x2), dzl=1)
    return (own,), (z1,), (x1_low, x1_high), (x1z1,), x2, (x2z1,), (x3_low, x3_high), (x3z1,)


def gather_item(pair):
    ys = [pair] + [shift(pair, dy=i) for i in (1, 2, 3)]
    return ys + [shift(piece, dk=1) for piece in ys]


def place_pieces(amps_v, pieces):
    _, _, y, zh, k = here()
    for dk in range(2):
        for dy in range(4):
            for dz in range(2):
                at = ((zh ^ dz) * 8 + (y ^ dy) * 2 + (k ^ dk)) * 48
                amps_v[pl.ds(pl.multiple_of(at, 16), 48), :] = pieces[dk * 4 + dy][dz]


PARTS = (1, 1, 2, 1, 2, 1, 2, 1)


def ladder_kernel(*refs):
    pieces = refs[:8]
    keep, send, amps_v, fac_v, acc = refs[-5:]
    row, _, y, zh, k = here()
    place_pieces(amps_v, pieces)
    blocks, at = [], 8
    for count in PARTS:
        blocks.append([(part, q) for part in refs[at:at + count] for q in range(part.shape[0])])
        at += count
    for q in range(4):
        for j in range(8):
            part, i = blocks[j][q]
            fac_v[q, pl.ds(pl.multiple_of((row ^ j) * 96, 32), 96), :] = part[i]
        factor = fac_v[q]
        halfway = lax.dot_general(
            amps_v[...], factor, (((1,), (1,)), ((), ())), preferred_element_type=F32
        ).astype(BF16)
        part = jnp.dot(factor, halfway, preferred_element_type=F32)
        if q == 0:
            acc[...] = part
        else:
            acc[...] += part
    for b in range(8):
        to = ((b % 4) ^ y) * 2 + ((b // 4) ^ zh)
        keep[to] = acc[pl.ds(pl.multiple_of(b * 96 + k * 48, 16), 48), :]
        send[to] = acc[pl.ds(pl.multiple_of(b * 96 + (1 - k) * 48, 16), 48), :].astype(BF16)


def ladder_item(pieces, blocks):
    scratch = [pltpu.VMEM((768, 768), BF16), pltpu.VMEM((4, 768, 768), BF16), pltpu.VMEM((768, 768), F32)]
    outs = [((8,) + TILE, F32), ((8,) + TILE, BF16)]
    return call(ladder_kernel, outs, (*pieces, *[part for block in blocks for part in block]), scratch)


def core_kernel(keep, got, mine, y1, y2, y3):
    mine[...] = keep[:2] + got[:2].astype(F32)
    for i, out in ((1, y1), (2, y2), (3, y3)):
        out[...] = (keep[2 * i:2 * i + 2] + got[2 * i:2 * i + 2].astype(F32)).astype(BF16)


def ring_kernel(mine, y1, y2, y3, left, out):
    total = mine[...] + y1[...].astype(F32) + y2[...].astype(F32) + y3[...].astype(F32)
    left[...] = total[0]
    out[...] = total[1].astype(BF16)


def reduce_item(keep, send):
    pair = (2,) + TILE
    mine, *outs = call(core_kernel, [(pair, F32)] + [(pair, BF16)] * 3, (keep, shift(send, dk=1)))
    ys = [shift(out, dy=i + 1) for i, out in enumerate(outs)]
    left, out = call(ring_kernel, [(TILE, F32), (TILE, BF16)], (mine, *ys))
    return left, shift(out, dzh=1)


def finish_kernel(which, counts, pairs, occ, vir, amps, left, got, out):
    row, col, *_ = here()
    slot = row * 4
    if which == 1:
        plan = Plan(counts)
        owner, place = plan.source(row)
        slot = jnp.where(plan.borrows(row), owner * 4 + place, slot + 1)
    energy = occ[pairs[slot, 0]] + occ[pairs[slot, 1]]
    across = jnp.broadcast_to(vir[...], TILE)
    lane = lax.broadcasted_iota(I32, TILE, 1)
    mine = lane - lax.broadcasted_iota(I32, TILE, 0) == col * 48
    down = jnp.sum(jnp.where(mine, across, 0.0), axis=1, keepdims=True)
    denominator = (down + across) - energy
    t = amps[0].astype(F32)
    ladder = left[...] + got[...].astype(F32)
    out[...] = (t - (ladder + denominator * t) / (denominator + level_shift)).astype(BF16)


def pass_kernel(counts, *refs):
    results, out = refs[:4], refs[4]
    plan = Plan(counts)
    row = here()[0]
    for slot in (2, 3):
        worker = plan.helper(row ^ 1, slot) ^ row
        out[slot - 2] = results[0][...]
        for dx in (1, 2, 3):
            @pl.when(worker == 2 * dx)
            def _():
                out[slot - 2] = results[dx][...]


def place_kernel(counts, done_0, passed, *refs):
    results, out = refs[:4], refs[4]
    plan = Plan(counts)
    row = here()[0]
    count = choose(plan.count, row)
    zero = jnp.zeros(TILE, BF16)
    out[0] = done_0[...]
    out[1] = jnp.where(count >= 2, results[0][...], zero)
    for slot in (2, 3):
        worker = plan.helper(row, slot) ^ row
        out[slot] = jnp.where((count > slot) & ((worker & 1) == 1), passed[slot - 2], zero)
        for dx in range(4):
            @pl.when((count > slot) & (worker == 2 * dx))
            def _():
                out[slot] = results[dx][...]


def update(amplitudes, factors, counts, pair_index, occ_energy, vir_energy):
    vir = vir_energy.reshape(1, 768)
    pair_0 = jnp.stack([amplitudes[0], shift(amplitudes[0], dzh=1)])
    pair_1 = borrow(counts, amplitudes)
    blocks = gather_factors(factors)
    pieces_0 = gather_item(pair_0)
    pieces_1 = gather_item(pair_1)
    parts_1 = ladder_item(pieces_1, blocks)
    parts_0 = ladder_item(pieces_0, blocks)
    sums_1 = reduce_item(*parts_1)
    sums_0 = reduce_item(*parts_0)

    def finish(which, amps, sums):
        kernel = lambda *refs: finish_kernel(which, *refs)
        args = (counts, pair_index, occ_energy, vir, amps, *sums)
        return call(kernel, [(TILE, BF16)], args, smem=3)[0]

    done_1 = finish(1, pair_1, sums_1)
    results = [done_1] + [shift(done_1, dx=dx) for dx in (1, 2, 3)]
    passed = shift(call(pass_kernel, [((2,) + TILE, BF16)], (counts, *results), smem=1)[0], dzl=1)
    done_0 = finish(0, amplitudes, sums_0)
    return call(place_kernel, [((4,) + TILE, BF16)], (counts, done_0, passed, *results), smem=1)[0]


def solution(mesh):
    in_specs = (P("row", "col", None), P("col", "row", None), P(), P(), P(), P())
    out_specs = P("row", "col", None)
    return jax.shard_map(update, mesh=mesh, in_specs=in_specs, out_specs=out_specs, check_vma=False)
```

```python
import itertools

import jax
import jax.numpy as jnp
from jax import lax
from jax.experimental import pallas as pl
from jax.experimental.pallas import tpu as pltpu
from jax.sharding import PartitionSpec as P


level_shift = 1.0

DEVICES = list(itertools.product(range(4), range(4), range(2), range(2), range(2)))
BF16, F32, I32 = jnp.bfloat16, jnp.float32, jnp.int32
TILE = (48, 768)


def position(x, y, zh, zl, k):
    return (x * 2 + zl) * 16 + zh * 8 + y * 2 + k


def shift(array, dx=0, dy=0, dzh=0, dzl=0, dk=0):
    pairs = [
        (position(x, y, zh, zl, k), position(x ^ dx, y ^ dy, zh ^ dzh, zl ^ dzl, k ^ dk))
        for x, y, zh, zl, k in DEVICES
    ]
    return lax.ppermute(array, ("row", "col"), pairs)


def call(kernel, outs, args, scratch=(), smem=0):
    spaces = [pltpu.SMEM] * smem + [pltpu.VMEM] * (len(args) - smem)
    return pl.pallas_call(
        kernel,
        out_shape=tuple(jax.ShapeDtypeStruct(s, d) for s, d in outs),
        in_specs=[pl.BlockSpec(memory_space=space) for space in spaces],
        out_specs=tuple(pl.BlockSpec(memory_space=pltpu.VMEM) for _ in outs),
        scratch_shapes=list(scratch),
        compiler_params=pltpu.CompilerParams(vmem_limit_bytes=40 << 20),
    )(*args)


def here():
    row = lax.axis_index("row").astype(I32)
    col = lax.axis_index("col").astype(I32)
    return row, col, (col // 2) % 4, col // 8, col % 2


def choose(values, index):
    out = values[0]
    for i in range(1, len(values)):
        out = jnp.where(index == i, values[i], out)
    return out


class Plan:
    def __init__(self, counts):
        self.count = [counts[i] for i in range(8)]
        self.extra = [jnp.maximum(c - 2, 0) for c in self.count]
        self.spare = [jnp.maximum(2 - c, 0) for c in self.count]
        self.extra_from, self.spare_from = [jnp.int32(0)], [jnp.int32(0)]
        for i in range(7):
            self.extra_from.append(self.extra_from[i] + self.extra[i])
            self.spare_from.append(self.spare_from[i] + self.spare[i])

    def borrows(self, row):
        return choose(self.count, row) < 2

    def source(self, row):
        wanted = choose(self.spare_from, row)
        owner = jnp.int32(0)
        for i in range(8):
            owner += (self.extra_from[i] + self.extra[i] <= wanted).astype(I32)
        owner = jnp.minimum(owner, 7)
        return owner, 2 + wanted - choose(self.extra_from, owner)

    def helper(self, row, slot):
        wanted = choose(self.extra_from, row) + (slot - 2)
        worker = jnp.int32(0)
        for i in range(8):
            worker += (self.spare_from[i] + self.spare[i] <= wanted).astype(I32)
        return jnp.minimum(worker, 7)


ROWS = ("near", "mine", "far", "pass2", "pass3", "energy", "own", "hop2", "local2", "hop3", "local3")
WIDTH = {"near": 4, "mine": 4, "pass2": 4, "pass3": 4, "energy": 2, "local2": 4, "local3": 4}
START = {name: sum(WIDTH.get(n, 1) for n in ROWS[:i]) for i, name in enumerate(ROWS)}
TABLE = (40, 768)


class Table:
    def __init__(self, ref):
        self.ref = ref

    def put(self, name, i, value):
        at = START[name] + i
        if value.dtype == jnp.bool_:
            value = jnp.where(value, jnp.float32(1), jnp.float32(0))
        self.ref[at:at + 1, :] = jnp.full((1, 768), value, F32)

    def row(self, name, i=0):
        return self.ref[START[name] + i:START[name] + i + 1, :]

    def flag(self, name, i=0):
        return self.row(name, i) > 0.5

    def pick(self, name, refs, otherwise):
        out = otherwise.astype(F32)
        for i, ref in enumerate(refs):
            out = jnp.where(self.flag(name, i), ref.astype(F32), out)
        return out.astype(BF16)


def offer_kernel(counts, pairs, occ, amps, *refs):
    outs, table = refs[:4], Table(refs[4])
    plan = Plan(counts)
    row = here()[0]
    for j in range(8):
        late = choose(plan.spare_from, row ^ j) - choose(plan.extra_from, row) == 1
        outs[j // 2][j % 2] = jnp.where(late, amps[3], amps[2])
    count, borrows = choose(plan.count, row), plan.borrows(row)
    owner, place = plan.source(row)
    source, step = owner ^ row, plan.source(row ^ 1)[0] ^ row
    for dx in range(4):
        table.put("near", dx, step >> 1 == dx)
        table.put("mine", dx, borrows & (source == 2 * dx))
    table.put("far", 0, borrows & ((source & 1) == 1))
    table.put("own", 0, count >= 2)
    for slot in (2, 3):
        there, worker = plan.helper(row ^ 1, slot) ^ row, plan.helper(row, slot) ^ row
        table.put(f"hop{slot}", 0, (count > slot) & ((worker & 1) == 1))
        for dx in range(4):
            table.put(f"pass{slot}", dx, there == 2 * dx)
            table.put(f"local{slot}", dx, (count > slot) & (worker == 2 * dx))
    for i, slot in enumerate((row * 4, jnp.where(borrows, owner * 4 + place, row * 4 + 1))):
        table.put("energy", i, occ[pairs[slot, 0]] + occ[pairs[slot, 1]])


def relay_kernel(table, amps, *refs):
    got, (relayed, mine), table = refs[:4], refs[4:], Table(table)
    relayed[...] = table.pick("near", [ref[1] for ref in got], got[0][1])
    mine[...] = table.pick("mine", [ref[0] for ref in got], amps[1])


def accept_kernel(table, mine, beside, relayed, relayed_beside, pair):
    table = Table(table)
    pair[0] = table.pick("far", [relayed[...]], mine[...])
    pair[1] = table.pick("far", [relayed_beside[...]], beside[...])


def borrow(scalars, amplitudes):
    outs = [((2,) + TILE, BF16)] * 4 + [(TABLE, F32)]
    *offers, table = call(offer_kernel, outs, (*scalars, amplitudes), smem=3)
    got = [offers[0]] + [shift(offers[dx], dx=dx) for dx in (1, 2, 3)]
    relayed, mine = call(relay_kernel, [(TILE, BF16)] * 2, (table, amplitudes, *got))
    near = shift(relayed, dzl=1)
    beside = shift(mine, dzh=1)
    far = shift(relayed, dzl=1, dzh=1)
    return call(accept_kernel, [((2,) + TILE, BF16)], (table, mine, beside, near, far))[0], table


def gather_factors(own):
    x3_low = shift(own[:2], dx=3)
    x1_high = shift(own[2:], dx=1)
    z1 = shift(own, dzl=1)
    x2 = shift(x3_low, dx=1), shift(x1_high, dx=3)
    x1_low = shift(own[:2], dx=1)
    x3_high = shift(own[2:], dx=3)
    x1z1 = shift(z1, dx=1)
    x3z1 = shift(z1, dx=3)
    x2z1 = shift(jnp.concatenate(x2), dzl=1)
    return (own,), (z1,), (x1_low, x1_high), (x1z1,), x2, (x2z1,), (x3_low, x3_high), (x3z1,)


def gather_item(pair):
    ys = [pair] + [shift(pair, dy=i) for i in (1, 2, 3)]
    return ys + [shift(piece, dk=1) for piece in ys]


def place_pieces(amps_v, pieces):
    _, _, y, zh, k = here()
    for dk in range(2):
        for dy in range(4):
            for dz in range(2):
                at = ((zh ^ dz) * 8 + (y ^ dy) * 2 + (k ^ dk)) * 48
                amps_v[pl.ds(pl.multiple_of(at, 16), 48), :] = pieces[dk * 4 + dy][dz]


PARTS = (1, 1, 2, 1, 2, 1, 2, 1)


def ladder_kernel(*refs):
    pieces = refs[:8]
    keep, send, amps_v, fac_v, acc = refs[-5:]
    row, _, y, zh, k = here()
    place_pieces(amps_v, pieces)
    blocks, at = [], 8
    for count in PARTS:
        blocks.append([(part, q) for part in refs[at:at + count] for q in range(part.shape[0])])
        at += count
    for q in range(4):
        for j in range(8):
            part, i = blocks[j][q]
            fac_v[q, pl.ds(pl.multiple_of((row ^ j) * 96, 32), 96), :] = part[i]
        factor = fac_v[q]
        halfway = lax.dot_general(
            amps_v[...], factor, (((1,), (1,)), ((), ())), preferred_element_type=F32
        ).astype(BF16)
        part = jnp.dot(factor, halfway, preferred_element_type=F32)
        if q == 0:
            acc[...] = part
        else:
            acc[...] += part
    for b in range(8):
        to = ((b % 4) ^ y) * 2 + ((b // 4) ^ zh)
        keep[to] = acc[pl.ds(pl.multiple_of(b * 96 + k * 48, 16), 48), :]
        send[to] = acc[pl.ds(pl.multiple_of(b * 96 + (1 - k) * 48, 16), 48), :].astype(BF16)


def ladder_item(pieces, blocks):
    scratch = [pltpu.VMEM((768, 768), BF16), pltpu.VMEM((4, 768, 768), BF16), pltpu.VMEM((768, 768), F32)]
    outs = [((8,) + TILE, F32), ((8,) + TILE, BF16)]
    return call(ladder_kernel, outs, (*pieces, *[part for block in blocks for part in block]), scratch)


def core_kernel(keep, got, mine, y1, y2, y3):
    mine[...] = keep[:2] + got[:2].astype(F32)
    for i, out in ((1, y1), (2, y2), (3, y3)):
        out[...] = (keep[2 * i:2 * i + 2] + got[2 * i:2 * i + 2].astype(F32)).astype(BF16)


def ring_kernel(mine, y1, y2, y3, left, out):
    total = mine[...] + y1[...].astype(F32) + y2[...].astype(F32) + y3[...].astype(F32)
    left[...] = total[0]
    out[...] = total[1].astype(BF16)


def reduce_item(keep, send):
    pair = (2,) + TILE
    mine, *outs = call(core_kernel, [(pair, F32)] + [(pair, BF16)] * 3, (keep, shift(send, dk=1)))
    ys = [shift(out, dy=i + 1) for i, out in enumerate(outs)]
    left, out = call(ring_kernel, [(TILE, F32), (TILE, BF16)], (mine, *ys))
    return left, shift(out, dzh=1)


def updated(table, item, vir, amps, ladder):
    col = here()[1]
    across = jnp.broadcast_to(vir[...], TILE)
    lane = lax.broadcasted_iota(I32, TILE, 1)
    mine = lane - lax.broadcasted_iota(I32, TILE, 0) == col * 48
    down = jnp.sum(jnp.where(mine, across, 0.0), axis=1, keepdims=True)
    denominator = (down + across) - table.row("energy", item)
    t = amps[0].astype(F32)
    return (t - (ladder + denominator * t) / (denominator + level_shift)).astype(BF16)


def finish_kernel(table, vir, amps, left, got, out):
    out[...] = updated(Table(table), 1, vir, amps, left[...] + got[...].astype(F32))


def pass_kernel(table, *refs):
    results, out = [ref[...] for ref in refs[:4]], refs[4]
    for slot in (2, 3):
        out[slot - 2] = Table(table).pick(f"pass{slot}", results, results[0])


def place_kernel(table, vir, amps, left, got, passed, *refs):
    results, out, table = [ref[...] for ref in refs[:4]], refs[4], Table(table)
    out[0] = updated(table, 0, vir, amps, left[...] + got[...].astype(F32))
    zero = jnp.zeros(TILE, BF16)
    out[1] = table.pick("own", results[:1], zero)
    for slot in (2, 3):
        hop = table.pick(f"hop{slot}", [passed[slot - 2]], zero)
        out[slot] = table.pick(f"local{slot}", results, hop)


def update(amplitudes, factors, counts, pair_index, occ_energy, vir_energy):
    vir = vir_energy.reshape(1, 768)
    pair_0 = jnp.stack([amplitudes[0], shift(amplitudes[0], dzh=1)])
    pair_1, table = borrow((counts, pair_index, occ_energy), amplitudes)
    blocks = gather_factors(factors)
    pieces_0 = gather_item(pair_0)
    pieces_1 = gather_item(pair_1)
    parts_1 = ladder_item(pieces_1, blocks)
    parts_0 = ladder_item(pieces_0, blocks)
    sums_1 = reduce_item(*parts_1)
    sums_0 = reduce_item(*parts_0)

    done_1 = call(finish_kernel, [(TILE, BF16)], (table, vir, pair_1, *sums_1))[0]
    results = [done_1] + [shift(done_1, dx=dx) for dx in (1, 2, 3)]
    passed = call(pass_kernel, [((2,) + TILE, BF16)], (table, *results))[0]
    passed = shift(passed, dzl=1)
    args = (table, vir, amplitudes, *sums_0, passed, *results)
    return call(place_kernel, [((4,) + TILE, BF16)], args)[0]


def solution(mesh):
    in_specs = (P("row", "col", None), P("col", "row", None), P(), P(), P(), P())
    out_specs = P("row", "col", None)
    return jax.shard_map(update, mesh=mesh, in_specs=in_specs, out_specs=out_specs, check_vma=False)
```
